32 devices in a mesh: groups: 2 (over y), wide: 8 (over z, x), narrow: 2 (over core).
Axes of the slice: x: 2, y: 2, z: 4, core: 2. Of those that a mesh axis runs over, the one named last changes fastest.
Arguments:
- states: bfloat16 [2048, 32, 256], P(None, ('groups', 'wide', 'narrow')), parts along dimension 1, may hold values from -6 to 6
- var_weights: bfloat16 [4, 256, 256], replicated, may hold values from -0.375 to 0.375
- samp_weights: bfloat16 [4, 256, 256], replicated, may hold values from -0.375 to 0.375
- norm_gains: float32 [3, 256], replicated, may hold values from 0.25 to 1.75
- edge_weights: bfloat16 [2, 256, 256], replicated, may hold values from -0.375 to 0.375
- none_weight: bfloat16 [256], replicated, may hold values from -0.375 to 0.375
Outputs:
- edge_prob: float32 [6, 2048, 2048], P('groups', 'wide', 'narrow'), parts along dimension 0
The draws below stay inside these ranges and needn't reach their ends.
There are 2 independent parts, one for each index of `groups`. The reference program is written for one: setup_inputs(seed, part) draws one part's arguments, and reference() takes and returns one part's arrays. A program takes and returns all parts, laid end to end along the dimension named above; an argument that names none is the same for every part. Nothing has to cross between parts.
All inputs are finite; a program needn't handle non-finite values.
Results may differ from the reference program's by a relative error of at most 0.015.
The reference program's roundings to bfloat16 on the way count: a program that leaves them out, or rounds other values in their place, can miss the bound.
Values may be sent and summed in bfloat16 or wider, within the bound.
A program may use at most 64 MiB of HBM per device.

```python
import jax
import jax.numpy as jnp
from jax import lax

V = 2048
D = 256
HEADS = 8
S = 16


def steps_of(rng, extent, cuts, low, top_value):
    factor_of, own = 1.0, jax.random.fold_in(rng, 6)
    for dim, blocks in cuts:
        draws = jnp.exp(jax.random.uniform(jax.random.fold_in(own, dim), (blocks,), jnp.float32, low / len(cuts), top_value / len(cuts)))
        factor_of = factor_of * jnp.repeat(draws, extent[dim] // blocks).reshape([-1 if axis == dim else 1 for axis in range(len(extent))])
    return factor_of


def normal_values(key, extent, deviation, most, pieces=(), kind=jnp.bfloat16):
    drawn = jax.random.normal(key, extent, jnp.float32) * deviation
    if len(pieces) > 0:
        drawn = steps_of(key, extent, pieces, -0.22, 0.18) * drawn
    return jnp.clip(drawn, min=-most, max=most).astype(kind)


def setup_inputs(seed: int = 0, part: int = 0) -> dict:
    key_list = jax.random.split(jax.random.key(seed), 7)
    own_keys = jax.random.split(jax.random.fold_in(key_list[6], part), 7)
    states = normal_values(own_keys[0], (V, S, D), 1.0, 6.0, ((1, 16),))
    var_weights = normal_values(key_list[1], (4, D, D), D ** -0.5, 0.375)
    samp_weights = normal_values(key_list[2], (4, D, D), D ** -0.5, 0.375)
    norm_gains = jnp.clip(1.0 + 0.15 * jax.random.normal(key_list[3], (3, D), jnp.float32), 0.25, 1.75)
    edge_weights = normal_values(key_list[4], (2, D, D), D ** -0.5, 0.375)
    none_weight = normal_values(key_list[5], (D,), D ** -0.5, 0.375)
    return dict(states=states, var_weights=var_weights, samp_weights=samp_weights, norm_gains=norm_gains, edge_weights=edge_weights, none_weight=none_weight)


def layer_norm(values, gain):
    mean = lax.optimization_barrier(jnp.mean(values, axis=-1, keepdims=True))
    centered = values - mean
    var = lax.optimization_barrier(jnp.mean(centered * centered, axis=-1, keepdims=True))
    return centered * lax.rsqrt(var + 1e-05) * gain

def project(normed, weight):
    return jnp.dot(normed, weight, preferred_element_type=jnp.float32).astype(jnp.bfloat16)

def attend(seq, gain, weights):
    length = seq.shape[0]
    normed = layer_norm(seq.astype(jnp.float32), gain).astype(jnp.bfloat16)
    queries = project(normed, weights[0]).reshape(length, HEADS, -1).astype(jnp.float32)
    keys_all = project(normed, weights[1]).reshape(length, HEADS, -1).astype(jnp.float32)
    values_all = project(normed, weights[2]).reshape(length, HEADS, -1).astype(jnp.float32)
    scale = 1.0 / queries.shape[2] ** 0.5
    scores = jnp.einsum('qhd,khd->hqk', queries, keys_all) * scale
    expd = jnp.exp(scores)
    probs = (expd / lax.optimization_barrier(jnp.sum(expd, axis=2, keepdims=True))).astype(jnp.bfloat16)
    mixed = jnp.einsum('hqk,khd->qhd', probs.astype(jnp.float32), values_all)
    mixed = mixed.reshape(length, -1).astype(jnp.bfloat16)
    update = jnp.dot(mixed, weights[3], preferred_element_type=jnp.float32)
    return (seq.astype(jnp.float32) + update).astype(jnp.bfloat16)

def reference(states, var_weights, samp_weights, norm_gains, edge_weights, none_weight):
    by_sample = jnp.transpose(states, (1, 0, 2))
    mixed_var = lax.map(lambda seq: attend(seq, norm_gains[0], var_weights), by_sample)
    by_variable = jnp.transpose(mixed_var, (1, 0, 2))
    mixed_samp = lax.map(lambda seq: attend(seq, norm_gains[1], samp_weights), by_variable)
    pooled = lax.optimization_barrier(jnp.max(mixed_samp, axis=1))
    normed = layer_norm(pooled.astype(jnp.float32), norm_gains[2]).astype(jnp.bfloat16)
    source = project(normed, edge_weights[0])
    target = project(normed, edge_weights[1])
    none_term = jnp.dot(normed, none_weight, preferred_element_type=jnp.float32).astype(jnp.bfloat16)
    escale = 1.0 / source.shape[1] ** 0.5
    forward = jnp.dot(source, target.T, preferred_element_type=jnp.float32) * escale
    backward = jnp.dot(target, source.T, preferred_element_type=jnp.float32) * escale
    absent = none_term.astype(jnp.float32)[:, None] + none_term.astype(jnp.float32)[None, :]
    expd = jnp.exp(jnp.stack([forward, backward, absent]))
    return expd / lax.optimization_barrier(jnp.sum(expd, axis=0, keepdims=True))
```

```python
import functools
import math

import jax
import jax.numpy as jnp
from jax import lax
from jax.experimental import pallas as pl
from jax.experimental.pallas import tpu as pltpu
from jax.sharding import PartitionSpec as P

HEADS = 8
BLOCK = 128
QUERIES = 256
KEYS = 256
F32, BF16, F8 = jnp.float32, jnp.bfloat16, jnp.float8_e4m3fn
PARTS = 4
PREPARE = 2
LAG = 1
MESH = pl.DeviceIdType.MESH


def layer_norm(values, gain):
    mean = jnp.mean(values, axis=-1, keepdims=True)
    centered = values - mean
    var = jnp.mean(centered * centered, axis=-1, keepdims=True)
    return (centered * lax.rsqrt(var + 1e-05) * gain).astype(BF16)


def project(normed, weight):
    return jnp.dot(normed, weight, preferred_element_type=F32).astype(BF16)


def across(a, b):
    return lax.dot_general(a, b, (((1,), (1,)), ((), ())), preferred_element_type=F32)


def attend_tokens(q, keys_of, values_of, length, same):
    width, tokens = q.shape
    size = width // HEADS
    step = min(KEYS, length)
    factor = math.log2(math.e) / math.sqrt(size)
    blank = jnp.zeros((size, tokens), BF16)
    stacked = jnp.concatenate(
        [
            jnp.concatenate([q[i * size : (i + 1) * size] if i == h else blank for h in range(HEADS)], axis=1)
            for i in range(HEADS)
        ],
        axis=0,
    )
    accs, total = None, None
    for j in range(0, length, step):
        scores = jnp.dot(keys_of(j, step), stacked, preferred_element_type=F32)
        expd = jnp.where(same, jnp.exp2(scores * factor), 0.0)
        part = jnp.sum(expd.reshape(step // 8, 8, HEADS * tokens), axis=0)
        total = part if total is None else total + part
        expd = expd.astype(BF16)
        values = values_of(j, step)
        terms = [
            jnp.dot(
                values[h * size : (h + 1) * size], expd[:, h * tokens : (h + 1) * tokens],
                preferred_element_type=F32,
            )
            for h in range(HEADS)
        ]
        accs = terms if accs is None else [acc + term for acc, term in zip(accs, terms)]
    inverse = 4.0 / jnp.sum(total, axis=0, keepdims=True)
    outs = [acc * inverse[:, h * tokens : (h + 1) * tokens] * 64.0 for h, acc in enumerate(accs)]
    return jnp.transpose(jnp.concatenate(outs, axis=0)).astype(BF16)


def low_part(values):
    return values - values.astype(F8).astype(F32)


def attend_across(q, keys, values):
    width, length = values.shape
    size = width // HEADS
    step = min(KEYS, length)
    factor = math.log2(math.e) / math.sqrt(size) / 4.0
    outs = []
    for h in range(HEADS):
        part = q[h * size : (h + 1) * size, :]
        high, low = part.astype(F8), low_part(part).astype(F8)
        stacked = jnp.concatenate([high, high, low, low], axis=0)
        pieces, total = [], None
        for j in range(0, length, step):
            scores = jnp.dot(keys[h, j : j + step, :], stacked, preferred_element_type=F32)
            expd = jnp.exp2(scores * factor)
            part = jnp.sum(expd.reshape(step // 8, 8, QUERIES), axis=0)
            total = part if total is None else total + part
            pieces.append(expd.astype(BF16))
        acc = jnp.dot(
            values[h * size : (h + 1) * size, :], jnp.concatenate(pieces, axis=0),
            preferred_element_type=F32,
        )
        outs.append(acc * (4.0 / jnp.sum(total, axis=0, keepdims=True)) * 64.0)
    return jnp.transpose(jnp.concatenate(outs, axis=0)).astype(BF16)


def mix_kernel(
    wide, narrow, x_ref, vw_ref, sw_ref, gain_ref, cols_ref, rows_ref,
    n_s, k_s, x_s, k8_s, vt_s, qt_s, kw_s, wt_s, outbox, inbox, pooled, mine,
    send_a, recv_a, send_c, recv_c, send_f, send_r, recv_r,
):
    total_vars, width = x_ref.shape
    devices = wide * narrow
    own = total_vars // devices
    per_block = QUERIES // own
    blocks = total_vars // QUERIES
    my_wide, my_narrow = lax.axis_index("wide"), lax.axis_index("narrow")
    me = my_wide * narrow + my_narrow

    def device(d):
        return {"wide": d // narrow, "narrow": lax.rem(d, narrow)}

    barrier = pltpu.get_barrier_semaphore()

    def greet(d, carry):
        @pl.when(d != me)
        def _():
            pl.semaphore_signal(barrier, inc=1, device_id=device(d), device_id_type=MESH)

        return carry

    lax.fori_loop(0, devices, greet, 0)

    size = width // HEADS
    spread = PARTS * size
    source = lax.broadcasted_iota(jnp.int32, (width, HEADS * spread), 0)
    column = lax.broadcasted_iota(jnp.int32, (width, HEADS * spread), 1)
    twice = jnp.where(source == column // spread * size + column % size, 2.0, 0.0)
    kw_s[...] = project(vw_ref[1], twice.astype(BF16))
    wt_s[0:width, :] = (jnp.transpose(vw_ref[0].astype(F32)) * 2.0).astype(BF16)
    wt_s[width : 2 * width, :] = jnp.transpose(vw_ref[2].astype(F32)).astype(BF16)
    odd = lax.broadcasted_iota(jnp.int32, (QUERIES, spread), 1) // size % 2 == 1

    def prepare(i, carry):
        rows = pl.ds(pl.multiple_of(i * QUERIES, QUERIES), QUERIES)
        normed = layer_norm(x_ref[rows, :].astype(F32), gain_ref[0:1, :])
        n_s[rows, :] = normed
        vt_s[:, rows] = (across(wt_s[width : 2 * width, :], normed) * 2.0**-8).astype(BF16)
        for h in range(HEADS):
            key = jnp.dot(normed, kw_s[:, h * spread : (h + 1) * spread], preferred_element_type=F32)
            k8_s[h, rows, :] = jnp.where(odd, low_part(key), key).astype(F8)
        return carry

    def prepare_some(i, carry):
        for u in range(PREPARE):
            prepare(i * PREPARE + u, carry)
        return carry

    lax.fori_loop(0, total_vars // QUERIES // PREPARE, prepare_some, 0)

    my_block = me // per_block

    def post(block):
        def one(j, carry):
            d = block * per_block + j

            @pl.when(d != me)
            def _():
                pltpu.make_async_remote_copy(
                    src_ref=outbox.at[d], dst_ref=inbox.at[me],
                    send_sem=send_a.at[d], recv_sem=recv_a.at[me],
                    device_id=device(d), device_id_type=MESH,
                ).start()

            return carry

        lax.fori_loop(0, per_block, one, 0)

    def block_of(t):
        block, bit = 0, 1
        while bit < blocks:
            block = block + bit * lax.rem(my_block // bit + (blocks - 1 - t) // bit, 2)
            bit *= 2
        return block

    def variable_block(t):
        block = block_of(t)
        rows = pl.ds(pl.multiple_of(block * QUERIES, QUERIES), QUERIES)
        out = attend_across(across(wt_s[0:width, :], n_s[rows, :]), k8_s, vt_s)
        update = jnp.dot(out, vw_ref[3], preferred_element_type=F32)
        mixed = x_ref[rows, :].astype(F32) + update
        outbox[pl.ds(block * per_block, per_block)] = mixed.reshape(per_block, own, width).astype(BF16)

    variable_block(0)
    pl.semaphore_wait(barrier, devices - 1)

    def variable_step(t, carry):
        post(block_of(t - 1))
        variable_block(t)
        return carry

    lax.fori_loop(1, blocks, variable_step, 0)
    if per_block > 1:
        post(my_block)
    inbox[me] = outbox[me]
    wt_s[0:width, :] = jnp.transpose(sw_ref[0].astype(F32)).astype(BF16)
    wt_s[width : 2 * width, :] = jnp.transpose(sw_ref[2].astype(F32)).astype(BF16)

    def collect(d, carry):
        @pl.when(d != me)
        def _():
            pltpu.make_async_remote_copy(
                src_ref=outbox.at[d], dst_ref=inbox.at[d],
                send_sem=send_a.at[d], recv_sem=recv_a.at[d],
                device_id=device(d), device_id_type=MESH,
            ).wait()

        return carry

    lax.fori_loop(0, devices, collect, 0)

    tile = 8 * devices
    lump = 16 if own % 16 == 0 else 8

    tiles = lump // 8

    def prepare_samples(i):
        if lump == own:
            values = inbox[...].astype(F32)
        else:
            values = inbox[:, pl.ds(pl.multiple_of(i * lump, lump), lump), :].astype(F32)
        rows = pl.ds(pl.multiple_of(i * tiles * tile, tiles * tile), tiles * tile)
        tokens = jnp.concatenate(
            [values[:, u * 8 : u * 8 + 8, :].reshape(tile, width) for u in range(tiles)], axis=0
        )
        x_s[rows, :] = tokens.astype(BF16)
        normed = layer_norm(tokens, gain_ref[1:2, :])
        k_s[rows, :] = project(normed, sw_ref[1])
        qt_s[:, rows] = across(wt_s[0:width, :], normed).astype(BF16)
        vt_s[:, rows] = (across(wt_s[width : 2 * width, :], normed) * 2.0**-8).astype(BF16)

    pooled[...] = jnp.full(pooled.shape, -jnp.inf, F32)
    step = min(KEYS, tile)
    row_var = lax.broadcasted_iota(jnp.int32, (step, HEADS * BLOCK), 0) % 8
    col_var = lax.broadcasted_iota(jnp.int32, (step, HEADS * BLOCK), 1) % 8
    same = row_var == col_var

    def sample_chunk(c):
        rows = pl.ds(pl.multiple_of(c * BLOCK, BLOCK), BLOCK)
        base = c // (tile // BLOCK)

        def among(a, n):
            return pl.ds(pl.multiple_of(base * tile + a, BLOCK), n)

        out = attend_tokens(
            qt_s[:, rows],
            lambda a, n: k_s[among(a, n), :],
            lambda a, n: vt_s[:, among(a, n)],
            tile, same,
        )
        update = jnp.dot(out, sw_ref[3], preferred_element_type=F32)
        mixed = (x_s[rows, :].astype(F32) + update).astype(BF16).astype(F32)
        best = jnp.max(mixed.reshape(BLOCK // 8, 8, width), axis=0)
        where = pl.ds(pl.multiple_of(base * 8, 8), 8)
        pooled[where, :] = jnp.maximum(pooled[where, :], best)

    piece = min(32, own)
    pieces = own // piece
    per_piece = piece * devices // BLOCK
    unroll = min(4, per_piece)
    half = devices // narrow
    target = me // half
    slot = lax.rem(me, half)
    column, pair = my_wide // 2, lax.rem(my_wide, 2)
    columns = wide // 2
    beside = {"wide": column * 2 + 1 - pair, "narrow": my_narrow}

    def piece_rows(g):
        return pl.ds(pl.multiple_of(g * piece, piece), piece)

    def to_column(w, rows, g):
        return pltpu.make_async_remote_copy(
            src_ref=mine.at[rows], dst_ref=cols_ref.at[slot, rows],
            send_sem=send_c.at[w], recv_sem=recv_c.at[slot, g],
            device_id={"wide": w * 2 + pair, "narrow": target}, device_id_type=MESH,
        )

    def to_pair(rows):
        return pltpu.make_async_remote_copy(
            src_ref=mine.at[rows], dst_ref=cols_ref.at[slot, rows],
            send_sem=send_c.at[columns], recv_sem=recv_c.at[slot, 0],
            device_id={"wide": column * 2 + 1 - pair, "narrow": target}, device_id_type=MESH,
        )

    def to_row(n, rows):
        return pltpu.make_async_remote_copy(
            src_ref=mine.at[rows], dst_ref=rows_ref.at[my_narrow, rows],
            send_sem=send_r.at[n], recv_sem=recv_r.at[my_narrow],
            device_id={"wide": my_wide, "narrow": n}, device_id_type=MESH,
        )

    def forward(i, rows):
        return pltpu.make_async_remote_copy(
            src_ref=cols_ref.at[i, rows], dst_ref=cols_ref.at[i, rows],
            send_sem=send_f.at[i], recv_sem=recv_c.at[i, 0],
            device_id=beside, device_id_type=MESH,
        )

    def arrival(i, rows, g):
        return pltpu.make_async_remote_copy(
            src_ref=cols_ref.at[i, rows], dst_ref=cols_ref.at[i, rows],
            send_sem=send_f.at[i], recv_sem=recv_c.at[i, g],
            device_id=beside, device_id_type=MESH,
        )

    def column_copies(do, rows, g):
        def one(w, carry):
            @pl.when(w != column)
            def _():
                do(to_column(w, rows, g))

            return carry

        lax.fori_loop(0, columns, one, 0)

    def chip_copies(do, rows):
        do(to_pair(rows))

        @pl.when(target != my_narrow)
        def _():
            do(to_column(column, rows, 0))

        def other(n, carry):
            @pl.when(n != my_narrow)
            def _():
                do(to_row(n, rows))

            return carry

        lax.fori_loop(0, narrow, other, 0)

    def each_source(do):
        def one(i, carry):
            from_wide = (my_narrow * half + i) // narrow
            passes_here = (lax.rem(from_wide, 2) == pair) & (from_wide // 2 != column)

            @pl.when(passes_here)
            def _():
                do(i)

            return carry

        lax.fori_loop(0, half, one, 0)

    def pass_on(g):
        rows = piece_rows(g)

        def one(i):
            arrival(i, rows, g).wait_recv()
            forward(i, rows).start()

        each_source(one)

    def sample_piece(g, carry):
        for i in range(piece // lump):
            prepare_samples(g * (piece // lump) + i)

        def group(i, inner):
            for u in range(unroll):
                sample_chunk(g * per_piece + i * unroll + u)
            return inner

        if per_piece == unroll:
            group(0, 0)
        else:
            lax.fori_loop(0, per_piece // unroll, group, 0)
        rows = piece_rows(g)
        best = layer_norm(pooled[rows, :], gain_ref[2:3, :])
        mine[rows, :] = best
        rows_ref[my_narrow, rows, :] = best

        @pl.when(target == my_narrow)
        def _():
            cols_ref[slot, rows, :] = best

        column_copies(lambda copy: copy.start(), rows, g)
        chip_copies(lambda copy: copy.start(), rows)

        @pl.when(g >= LAG)
        def _():
            pass_on(g - LAG)

        return carry

    lax.fori_loop(0, pieces, sample_piece, 0)
    lax.fori_loop(max(pieces - LAG, 0), pieces, lambda g, carry: (pass_on(g), carry)[1], 0)
    whole = pl.ds(0, own)

    def arrived(i, carry):
        from_wide = (my_narrow * half + i) // narrow
        passes_here = (lax.rem(from_wide, 2) == pair) & (from_wide // 2 != column)

        @pl.when(jnp.logical_not(passes_here) & (my_narrow * half + i != me))
        def _():
            arrival(i, whole, 0).wait_recv()

        return carry

    lax.fori_loop(0, half, arrived, 0)

    def row_arrived(n, carry):
        @pl.when(n != my_narrow)
        def _():
            pltpu.make_async_remote_copy(
                src_ref=mine, dst_ref=rows_ref.at[n], send_sem=send_r.at[0],
                recv_sem=recv_r.at[n], device_id=beside, device_id_type=MESH,
            ).wait_recv()

        return carry

    lax.fori_loop(0, narrow, row_arrived, 0)
    column_copies(lambda copy: copy.wait_send(), whole, 0)
    chip_copies(lambda copy: copy.wait_send(), whole)
    each_source(lambda i: forward(i, whole).wait_send())


def edge_kernel(rows_ref, cols_ref, w_ref, none_ref, out_ref, src_s, dst_s, none_s):
    scale = 1.0 / rows_ref.shape[1] ** 0.5
    none = jnp.broadcast_to(none_ref[...][None, :], (16, rows_ref.shape[1]))

    @pl.when(pl.program_id(0) == 0)
    def _():
        rows = rows_ref[...]
        src_s[...] = project(rows, w_ref[0])
        dst_s[...] = project(rows, w_ref[1])
        none_s[...] = across(rows, none).astype(BF16).astype(F32)

    cols = cols_ref[...]
    forward = jnp.exp(across(src_s[...], project(cols, w_ref[1])) * scale)
    backward = jnp.exp(across(dst_s[...], project(cols, w_ref[0])) * scale)
    none_cols = across(none, cols).astype(BF16).astype(F32)
    absent = jnp.exp(none_s[:, 0:1] + none_cols[0:1, :])
    total = forward + backward + absent
    out_ref[0] = forward / total
    out_ref[1] = backward / total
    out_ref[2] = absent / total


def on_device(states, var_weights, samp_weights, norm_gains, edge_weights, none_weight):
    total_vars, samp_local, width = states.shape
    wide, narrow = lax.axis_size("wide"), lax.axis_size("narrow")
    devices = wide * narrow
    own = total_vars // devices
    assert samp_local == 1 and BLOCK % own == 0 and own % 8 == 0
    half = devices // narrow
    assert narrow == 2 and wide % 2 == 0 and half % 4 == 0
    spread = PARTS * (width // HEADS)
    piece = min(32, own)
    vmem = pl.BlockSpec(memory_space=pltpu.VMEM)
    dma = pltpu.SemaphoreType.DMA
    cols, rows = pl.pallas_call(
        functools.partial(mix_kernel, wide, narrow),
        out_shape=(
            jax.ShapeDtypeStruct((half, own, width), BF16),
            jax.ShapeDtypeStruct((narrow, own, width), BF16),
        ),
        in_specs=[vmem] * 4,
        out_specs=(vmem, vmem),
        scratch_shapes=[pltpu.VMEM((total_vars, width), BF16)] * 3
        + [
            pltpu.VMEM((HEADS, total_vars, spread), F8),
            pltpu.VMEM((width, total_vars), BF16),
            pltpu.VMEM((width, total_vars), BF16),
            pltpu.VMEM((width, HEADS * spread), BF16),
            pltpu.VMEM((2 * width, width), BF16),
            pltpu.VMEM((devices, own, width), BF16),
            pltpu.VMEM((devices, own, width), BF16),
            pltpu.VMEM((own, width), F32),
            pltpu.VMEM((own, width), BF16),
            dma((devices,)), dma((devices,)), dma((wide // 2 + 1,)), dma((half, own // piece)),
            dma((half,)), dma((narrow,)), dma((narrow,)),
        ],
        compiler_params=pltpu.CompilerParams(
            collective_id=0, has_side_effects=True, vmem_limit_bytes=60 * 2**20
        ),
        name="mix",
    )(states.reshape(total_vars, width), var_weights, samp_weights, norm_gains)
    cols = cols.reshape(half * own, width)
    rows = rows.reshape(narrow * own, width)
    row_count, col_count = narrow * own, half * own
    tile = min(256, col_count)
    return pl.pallas_call(
        edge_kernel,
        grid=(col_count // tile,),
        out_shape=jax.ShapeDtypeStruct((3, row_count, col_count), F32),
        in_specs=[
            pl.BlockSpec((row_count, width), lambda i: (0, 0)),
            pl.BlockSpec((tile, width), lambda i: (i, 0)),
            pl.BlockSpec((2, width, width), lambda i: (0, 0, 0)),
            pl.BlockSpec((width,), lambda i: (0,)),
        ],
        out_specs=pl.BlockSpec((3, row_count, tile), lambda i: (0, 0, i)),
        scratch_shapes=[
            pltpu.VMEM((row_count, width), BF16),
            pltpu.VMEM((row_count, width), BF16),
            pltpu.VMEM((row_count, 16), F32),
        ],
        name="edge",
    )(rows, cols, edge_weights, none_weight)


def solution(mesh):
    return jax.shard_map(
        on_device,
        mesh=mesh,
        in_specs=(P(None, ("groups", "wide", "narrow"), None), P(), P(), P(), P(), P()),
        out_specs=P("groups", "wide", "narrow"),
        check_vma=False,
    )
```

```python
import functools
import math

import jax
import jax.numpy as jnp
from jax import lax
from jax.experimental import pallas as pl
from jax.experimental.pallas import tpu as pltpu
from jax.sharding import PartitionSpec as P

HEADS = 8
BLOCK = 128
QUERIES = 256
KEYS = 256
ACROSS = 2048
F32, BF16, F8 = jnp.float32, jnp.bfloat16, jnp.float8_e4m3fn
PARTS = 4
PREPARE = 2
LAG = 2
MESH = pl.DeviceIdType.MESH


def layer_norm(values, gain):
    mean = jnp.mean(values, axis=-1, keepdims=True)
    centered = values - mean
    var = jnp.mean(centered * centered, axis=-1, keepdims=True)
    return (centered * lax.rsqrt(var + 1e-05) * gain).astype(BF16)


def project(normed, weight):
    return jnp.dot(normed, weight, preferred_element_type=F32).astype(BF16)


def across(a, b):
    return lax.dot_general(a, b, (((1,), (1,)), ((), ())), preferred_element_type=F32)


def attend_tokens(q, keys_of, values_of, length, same):
    width, tokens = q.shape
    size = width // HEADS
    step = min(KEYS, length)
    factor = math.log2(math.e) / math.sqrt(size)
    blank = jnp.zeros((size, tokens), BF16)
    stacked = jnp.concatenate(
        [
            jnp.concatenate([q[i * size : (i + 1) * size] if i == h else blank for h in range(HEADS)], axis=1)
            for i in range(HEADS)
        ],
        axis=0,
    )
    accs, total = None, None
    for j in range(0, length, step):
        scores = jnp.dot(keys_of(j, step), stacked, preferred_element_type=F32)
        expd = jnp.where(same, jnp.exp2(scores * factor), 0.0)
        part = jnp.sum(expd.reshape(step // 8, 8, HEADS * tokens), axis=0)
        total = part if total is None else total + part
        expd = expd.astype(BF16)
        values = values_of(j, step)
        terms = [
            jnp.dot(
                values[h * size : (h + 1) * size], expd[:, h * tokens : (h + 1) * tokens],
                preferred_element_type=F32,
            )
            for h in range(HEADS)
        ]
        accs = terms if accs is None else [acc + term for acc, term in zip(accs, terms)]
    inverse = 4.0 / jnp.sum(total, axis=0, keepdims=True)
    outs = [acc * inverse[:, h * tokens : (h + 1) * tokens] * 64.0 for h, acc in enumerate(accs)]
    return jnp.transpose(jnp.concatenate(outs, axis=0)).astype(BF16)


def low_part(values):
    return values - values.astype(F8).astype(F32)


def attend_across(q, keys, values):
    width, length = values.shape
    size = width // HEADS
    step = min(ACROSS, length)
    factor = math.log2(math.e) / math.sqrt(size) / 4.0
    outs = []
    for h in range(HEADS):
        part = q[h * size : (h + 1) * size, :]
        high, low = part.astype(F8), low_part(part).astype(F8)
        stacked = jnp.concatenate([high, high, low, low], axis=0)
        pieces, total = [], None
        for j in range(0, length, step):
            scores = jnp.dot(keys[h, j : j + step, :], stacked, preferred_element_type=F32)
            expd = jnp.exp2(scores * factor)
            part = jnp.sum(expd.reshape(step // 8, 8, QUERIES), axis=0)
            total = part if total is None else total + part
            pieces.append(expd.astype(BF16))
        acc = jnp.dot(
            values[h * size : (h + 1) * size, :], jnp.concatenate(pieces, axis=0),
            preferred_element_type=F32,
        )
        outs.append(acc * (4.0 / jnp.sum(total, axis=0, keepdims=True)) * 64.0)
    return jnp.transpose(jnp.concatenate(outs, axis=0)).astype(BF16)


def mix_kernel(
    wide, narrow, x_ref, vw_ref, sw_ref, gain_ref, cols_ref, rows_ref,
    n_s, k_s, x_s, k8_s, vt_s, qt_s, kw_s, wt_s, outbox, inbox, pooled, mine,
    send_a, recv_a, send_c, recv_c, send_f, send_r, recv_r,
):
    total_vars, width = x_ref.shape
    devices = wide * narrow
    own = total_vars // devices
    per_block = QUERIES // own
    blocks = total_vars // QUERIES
    my_wide, my_narrow = lax.axis_index("wide"), lax.axis_index("narrow")
    me = my_wide * narrow + my_narrow

    def device(d):
        return {"wide": d // narrow, "narrow": lax.rem(d, narrow)}

    barrier = pltpu.get_barrier_semaphore()

    def greet(d, carry):
        @pl.when(d != me)
        def _():
            pl.semaphore_signal(barrier, inc=1, device_id=device(d), device_id_type=MESH)

        return carry

    lax.fori_loop(0, devices, greet, 0)

    size = width // HEADS
    spread = PARTS * size
    source = lax.broadcasted_iota(jnp.int32, (width, HEADS * spread), 0)
    column = lax.broadcasted_iota(jnp.int32, (width, HEADS * spread), 1)
    twice = jnp.where(source == column // spread * size + column % size, 2.0, 0.0)
    kw_s[...] = project(vw_ref[1], twice.astype(BF16))
    wt_s[0:width, :] = (jnp.transpose(vw_ref[0].astype(F32)) * 2.0).astype(BF16)
    wt_s[width : 2 * width, :] = jnp.transpose(vw_ref[2].astype(F32)).astype(BF16)
    odd = lax.broadcasted_iota(jnp.int32, (QUERIES, spread), 1) // size % 2 == 1

    def prepare(i, carry):
        rows = pl.ds(pl.multiple_of(i * QUERIES, QUERIES), QUERIES)
        normed = layer_norm(x_ref[rows, :].astype(F32), gain_ref[0:1, :])
        n_s[rows, :] = normed
        vt_s[:, rows] = (across(wt_s[width : 2 * width, :], normed) * 2.0**-8).astype(BF16)
        for h in range(HEADS):
            key = jnp.dot(normed, kw_s[:, h * spread : (h + 1) * spread], preferred_element_type=F32)
            k8_s[h, rows, :] = jnp.where(odd, low_part(key), key).astype(F8)
        return carry

    def prepare_some(i, carry):
        for u in range(PREPARE):
            prepare(i * PREPARE + u, carry)
        return carry

    lax.fori_loop(0, total_vars // QUERIES // PREPARE, prepare_some, 0)

    my_block = me // per_block

    def block_of(t):
        block, bit = 0, 1
        while bit < blocks:
            block = block + bit * lax.rem(my_block // bit + (blocks - 1 - t) // bit, 2)
            bit *= 2
        return block

    def rows_of(block):
        return pl.ds(pl.multiple_of(block * QUERIES, QUERIES), QUERIES)

    def send(d):
        pltpu.make_async_remote_copy(
            src_ref=outbox.at[d], dst_ref=inbox.at[me],
            send_sem=send_a.at[d], recv_sem=recv_a.at[me],
            device_id=device(d), device_id_type=MESH,
        ).start()

    def post(block):
        if per_block <= 4:
            for j in range(per_block):
                send(block * per_block + j)
        else:
            lax.fori_loop(0, per_block, lambda j, carry: (send(block * per_block + j), carry)[1], 0)

    def variable_block(t):
        block = block_of(t)
        rows = rows_of(block)
        out = attend_across(across(wt_s[0:width, :], n_s[rows, :]), k8_s, vt_s)
        update = jnp.dot(out, vw_ref[3], preferred_element_type=F32)
        mixed = x_ref[rows, :].astype(F32) + update
        outbox[pl.ds(block * per_block, per_block)] = mixed.reshape(per_block, own, width).astype(BF16)

    variable_block(0)
    pl.semaphore_wait(barrier, devices - 1)

    def variable_step(t, carry):
        post(block_of(t - 1))
        variable_block(t)
        return carry

    lax.fori_loop(1, blocks, variable_step, 0)

    def post_own(j, carry):
        d = my_block * per_block + j

        @pl.when(d != me)
        def _():
            send(d)

        return carry

    lax.fori_loop(0, per_block, post_own, 0)
    inbox[me] = outbox[me]
    wt_s[0:width, :] = jnp.transpose(sw_ref[0].astype(F32)).astype(BF16)
    wt_s[width : 2 * width, :] = jnp.transpose(sw_ref[2].astype(F32)).astype(BF16)

    def collect(d, carry):
        @pl.when(d != me)
        def _():
            pltpu.make_async_remote_copy(
                src_ref=outbox.at[d], dst_ref=inbox.at[d],
                send_sem=send_a.at[d], recv_sem=recv_a.at[d],
                device_id=device(d), device_id_type=MESH,
            ).wait()

        return carry

    lax.fori_loop(0, devices, collect, 0)

    tile = 8 * devices
    lump = 16 if own % 16 == 0 else 8

    tiles = lump // 8

    def prepare_samples(i):
        if lump == own:
            values = inbox[...].astype(F32)
        else:
            values = inbox[:, pl.ds(pl.multiple_of(i * lump, lump), lump), :].astype(F32)
        rows = pl.ds(pl.multiple_of(i * tiles * tile, tiles * tile), tiles * tile)
        tokens = jnp.concatenate(
            [values[:, u * 8 : u * 8 + 8, :].reshape(tile, width) for u in range(tiles)], axis=0
        )
        x_s[rows, :] = tokens.astype(BF16)
        normed = layer_norm(tokens, gain_ref[1:2, :])
        k_s[rows, :] = project(normed, sw_ref[1])
        qt_s[:, rows] = across(wt_s[0:width, :], normed).astype(BF16)
        vt_s[:, rows] = (across(wt_s[width : 2 * width, :], normed) * 2.0**-8).astype(BF16)

    pooled[...] = jnp.full(pooled.shape, -jnp.inf, F32)
    step = min(KEYS, tile)
    row_var = lax.broadcasted_iota(jnp.int32, (step, HEADS * BLOCK), 0) % 8
    col_var = lax.broadcasted_iota(jnp.int32, (step, HEADS * BLOCK), 1) % 8
    same = row_var == col_var

    def sample_chunk(c):
        rows = pl.ds(pl.multiple_of(c * BLOCK, BLOCK), BLOCK)
        base = c // (tile // BLOCK)

        def among(a, n):
            return pl.ds(pl.multiple_of(base * tile + a, BLOCK), n)

        return attend_tokens(
            qt_s[:, rows],
            lambda a, n: k_s[among(a, n), :],
            lambda a, n: vt_s[:, among(a, n)],
            tile, same,
        )

    def sample_chunks(c, count):
        out = jnp.concatenate([sample_chunk(c + u) for u in range(count)], axis=0)
        update = jnp.dot(out, sw_ref[3], preferred_element_type=F32)
        rows = pl.ds(pl.multiple_of(c * BLOCK, BLOCK), count * BLOCK)
        mixed = (x_s[rows, :].astype(F32) + update).astype(BF16).astype(F32)
        best = jnp.max(mixed.reshape(count, BLOCK // 8, 8, width), axis=1)
        for u in range(count):
            where = pl.ds(pl.multiple_of((c + u) // (tile // BLOCK) * 8, 8), 8)
            pooled[where, :] = jnp.maximum(pooled[where, :], best[u])

    piece = min(32, own)
    pieces = own // piece
    per_piece = piece * devices // BLOCK
    unroll = min(4, per_piece)
    half = devices // narrow
    target = me // half
    slot = lax.rem(me, half)
    column, pair = my_wide // 2, lax.rem(my_wide, 2)
    columns = wide // 2
    beside = {"wide": column * 2 + 1 - pair, "narrow": my_narrow}

    def piece_rows(g):
        return pl.ds(pl.multiple_of(g * piece, piece), piece)

    def to_column(w, rows, g):
        return pltpu.make_async_remote_copy(
            src_ref=mine.at[rows], dst_ref=cols_ref.at[slot, rows],
            send_sem=send_c.at[w], recv_sem=recv_c.at[slot, g],
            device_id={"wide": w * 2 + pair, "narrow": target}, device_id_type=MESH,
        )

    def to_pair(rows):
        return pltpu.make_async_remote_copy(
            src_ref=mine.at[rows], dst_ref=cols_ref.at[slot, rows],
            send_sem=send_c.at[columns], recv_sem=recv_c.at[slot, 0],
            device_id={"wide": column * 2 + 1 - pair, "narrow": target}, device_id_type=MESH,
        )

    def to_row(n, rows):
        return pltpu.make_async_remote_copy(
            src_ref=mine.at[rows], dst_ref=rows_ref.at[my_narrow, rows],
            send_sem=send_r.at[n], recv_sem=recv_r.at[my_narrow],
            device_id={"wide": my_wide, "narrow": n}, device_id_type=MESH,
        )

    def forward(i, rows):
        return pltpu.make_async_remote_copy(
            src_ref=cols_ref.at[i, rows], dst_ref=cols_ref.at[i, rows],
            send_sem=send_f.at[i], recv_sem=recv_c.at[i, 0],
            device_id=beside, device_id_type=MESH,
        )

    def arrival(i, rows, g):
        return pltpu.make_async_remote_copy(
            src_ref=cols_ref.at[i, rows], dst_ref=cols_ref.at[i, rows],
            send_sem=send_f.at[i], recv_sem=recv_c.at[i, g],
            device_id=beside, device_id_type=MESH,
        )

    def column_copies(do, rows, g):
        def one(w, carry):
            @pl.when(w != column)
            def _():
                do(to_column(w, rows, g))

            return carry

        lax.fori_loop(0, columns, one, 0)

    def chip_copies(do, rows):
        do(to_pair(rows))

        @pl.when(target != my_narrow)
        def _():
            do(to_column(column, rows, 0))

        def other(n, carry):
            @pl.when(n != my_narrow)
            def _():
                do(to_row(n, rows))

            return carry

        lax.fori_loop(0, narrow, other, 0)

    def each_source(do):
        def one(i, carry):
            from_wide = (my_narrow * half + i) // narrow
            passes_here = (lax.rem(from_wide, 2) == pair) & (from_wide // 2 != column)

            @pl.when(passes_here)
            def _():
                do(i)

            return carry

        lax.fori_loop(0, half, one, 0)

    def pass_on(g):
        rows = piece_rows(g)

        def one(i):
            arrival(i, rows, g).wait_recv()
            forward(i, rows).start()

        each_source(one)

    def prepare_piece(g):
        for i in range(piece // lump):
            prepare_samples(g * (piece // lump) + i)

    def sample_piece(g, following):
        def group(i, inner):
            sample_chunks(g * per_piece + i * unroll, unroll)
            return inner

        if per_piece == unroll:
            group(0, 0)
        else:
            lax.fori_loop(0, per_piece // unroll, group, 0)
        if following:
            prepare_piece(g + 1)
        rows = piece_rows(g)
        best = layer_norm(pooled[rows, :], gain_ref[2:3, :])
        mine[rows, :] = best
        rows_ref[my_narrow, rows, :] = best

        @pl.when(target == my_narrow)
        def _():
            cols_ref[slot, rows, :] = best

        column_copies(lambda copy: copy.start(), rows, g)
        chip_copies(lambda copy: copy.start(), rows)

    def sample_step(g, carry):
        sample_piece(g, True)

        @pl.when(g >= LAG)
        def _():
            pass_on(g - LAG)

        return carry

    prepare_piece(0)
    if pieces > 1:
        lax.fori_loop(0, pieces - 1, sample_step, 0)
    sample_piece(pieces - 1, False)
    lax.fori_loop(max(pieces - 1 - LAG, 0), pieces, lambda g, carry: (pass_on(g), carry)[1], 0)
    whole = pl.ds(0, own)

    def arrived(i, carry):
        from_wide = (my_narrow * half + i) // narrow
        passes_here = (lax.rem(from_wide, 2) == pair) & (from_wide // 2 != column)

        @pl.when(jnp.logical_not(passes_here) & (my_narrow * half + i != me))
        def _():
            arrival(i, whole, 0).wait_recv()

        return carry

    lax.fori_loop(0, half, arrived, 0)

    def row_arrived(n, carry):
        @pl.when(n != my_narrow)
        def _():
            pltpu.make_async_remote_copy(
                src_ref=mine, dst_ref=rows_ref.at[n], send_sem=send_r.at[0],
                recv_sem=recv_r.at[n], device_id=beside, device_id_type=MESH,
            ).wait_recv()

        return carry

    lax.fori_loop(0, narrow, row_arrived, 0)
    column_copies(lambda copy: copy.wait_send(), whole, 0)
    chip_copies(lambda copy: copy.wait_send(), whole)
    each_source(lambda i: forward(i, whole).wait_send())


def edge_kernel(tile, rows_ref, cols_ref, w_ref, none_ref, out_ref, held, sem):
    width = rows_ref.shape[1]
    scale = 1.0 / width**0.5
    none = jnp.broadcast_to(none_ref[...][None, :], (16, width))
    rows = rows_ref[...]
    src = project(rows, w_ref[0])
    dst = project(rows, w_ref[1])
    none_rows = across(rows, none).astype(BF16).astype(F32)[:, 0:1]
    copies = []
    for i in range(0, cols_ref.shape[0], tile):
        cols = cols_ref[i : i + tile, :]
        forward = jnp.exp(across(src, project(cols, w_ref[1])) * scale)
        backward = jnp.exp(across(dst, project(cols, w_ref[0])) * scale)
        none_cols = across(none, cols).astype(BF16).astype(F32)
        absent = jnp.exp(none_rows + none_cols[0:1, :])
        total = forward + backward + absent
        lanes = pl.ds(i, tile)
        held[0, :, lanes] = forward / total
        held[1, :, lanes] = backward / total
        held[2, :, lanes] = absent / total
        copies.append(
            pltpu.make_async_copy(held.at[:, :, lanes], out_ref.at[:, :, lanes], sem.at[i // tile])
        )
        copies[-1].start()
    for copy in copies:
        copy.wait()


def on_device(states, var_weights, samp_weights, norm_gains, edge_weights, none_weight):
    total_vars, samp_local, width = states.shape
    wide, narrow = lax.axis_size("wide"), lax.axis_size("narrow")
    devices = wide * narrow
    own = total_vars // devices
    assert samp_local == 1 and BLOCK % own == 0 and own % 8 == 0
    half = devices // narrow
    assert narrow == 2 and wide % 2 == 0 and half % 4 == 0
    spread = PARTS * (width // HEADS)
    piece = min(32, own)
    vmem = pl.BlockSpec(memory_space=pltpu.VMEM)
    dma = pltpu.SemaphoreType.DMA
    cols, rows = pl.pallas_call(
        functools.partial(mix_kernel, wide, narrow),
        out_shape=(
            jax.ShapeDtypeStruct((half, own, width), BF16),
            jax.ShapeDtypeStruct((narrow, own, width), BF16),
        ),
        in_specs=[vmem] * 4,
        out_specs=(vmem, vmem),
        scratch_shapes=[pltpu.VMEM((total_vars, width), BF16)] * 3
        + [
            pltpu.VMEM((HEADS, total_vars, spread), F8),
            pltpu.VMEM((width, total_vars), BF16),
            pltpu.VMEM((width, total_vars), BF16),
            pltpu.VMEM((width, HEADS * spread), BF16),
            pltpu.VMEM((2 * width, width), BF16),
            pltpu.VMEM((devices, own, width), BF16),
            pltpu.VMEM((devices, own, width), BF16),
            pltpu.VMEM((own, width), F32),
            pltpu.VMEM((own, width), BF16),
            dma((devices,)), dma((devices,)), dma((wide // 2 + 1,)), dma((half, own // piece)),
            dma((half,)), dma((narrow,)), dma((narrow,)),
        ],
        compiler_params=pltpu.CompilerParams(
            collective_id=0, has_side_effects=True, vmem_limit_bytes=60 * 2**20
        ),
        name="mix",
    )(states.reshape(total_vars, width), var_weights, samp_weights, norm_gains)
    cols = cols.reshape(half * own, width)
    rows = rows.reshape(narrow * own, width)
    row_count, col_count = narrow * own, half * own
    tile = min(256, col_count)
    return pl.pallas_call(
        functools.partial(edge_kernel, tile),
        out_shape=jax.ShapeDtypeStruct((3, row_count, col_count), F32),
        in_specs=[vmem] * 4,
        out_specs=pl.BlockSpec(memory_space=pl.ANY),
        scratch_shapes=[pltpu.VMEM((3, row_count, col_count), F32), dma((col_count // tile,))],
        name="edge",
    )(rows, cols, edge_weights, none_weight)


def solution(mesh):
    return jax.shard_map(
        on_device,
        mesh=mesh,
        in_specs=(P(None, ("groups", "wide", "narrow"), None), P(), P(), P(), P(), P()),
        out_specs=P("groups", "wide", "narrow"),
        check_vma=False,
    )
```

```python
import functools
import math

import jax
import jax.numpy as jnp
from jax import lax
from jax.experimental import pallas as pl
from jax.experimental.pallas import tpu as pltpu
from jax.sharding import PartitionSpec as P

HEADS = 8
BLOCK = 128
QUERIES = 256
KEYS = 256
ACROSS = 2048
F32, BF16, F8 = jnp.float32, jnp.bfloat16, jnp.float8_e4m3fn
PARTS = 4
PREPARE = 4
LAG = 2
MESH = pl.DeviceIdType.MESH


def layer_norm(values, gain):
    mean = jnp.mean(values, axis=-1, keepdims=True)
    centered = values - mean
    var = jnp.mean(centered * centered, axis=-1, keepdims=True)
    return (centered * lax.rsqrt(var + 1e-05) * gain).astype(BF16)


def project(normed, weight):
    return jnp.dot(normed, weight, preferred_element_type=F32).astype(BF16)


def across(a, b):
    return lax.dot_general(a, b, (((1,), (1,)), ((), ())), preferred_element_type=F32)


def attend_tokens(q, keys_of, values_of, length, same):
    width, tokens = q.shape
    size = width // HEADS
    step = min(KEYS, length)
    factor = math.log2(math.e) / math.sqrt(size)
    blank = jnp.zeros((size, tokens), BF16)
    stacked = jnp.concatenate(
        [
            jnp.concatenate([q[i * size : (i + 1) * size] if i == h else blank for h in range(HEADS)], axis=1)
            for i in range(HEADS)
        ],
        axis=0,
    )
    accs, total = None, None
    for j in range(0, length, step):
        scores = jnp.dot(keys_of(j, step), stacked, preferred_element_type=F32)
        expd = jnp.where(same, jnp.exp2(scores * factor), 0.0)
        part = jnp.sum(expd.reshape(step // 8, 8, HEADS * tokens), axis=0)
        total = part if total is None else total + part
        expd = expd.astype(BF16)
        values = values_of(j, step)
        terms = [
            jnp.dot(
                values[h * size : (h + 1) * size], expd[:, h * tokens : (h + 1) * tokens],
                preferred_element_type=F32,
            )
            for h in range(HEADS)
        ]
        accs = terms if accs is None else [acc + term for acc, term in zip(accs, terms)]
    inverse = 4.0 / jnp.sum(total, axis=0, keepdims=True)
    outs = [acc * inverse[:, h * tokens : (h + 1) * tokens] * 64.0 for h, acc in enumerate(accs)]
    return jnp.transpose(jnp.concatenate(outs, axis=0)).astype(BF16)


def low_part(values):
    return values - values.astype(F8).astype(F32)


def attend_across(q, keys, values):
    width, length = values.shape
    size = width // HEADS
    step = min(ACROSS, length)
    factor = math.log2(math.e) / math.sqrt(size) / 4.0
    outs = []
    for h in range(HEADS):
        part = q[h * size : (h + 1) * size, :]
        high, low = part.astype(F8), low_part(part).astype(F8)
        stacked = jnp.concatenate([high, high, low, low], axis=0)
        pieces, total = [], None
        for j in range(0, length, step):
            scores = jnp.dot(keys[h, j : j + step, :], stacked, preferred_element_type=F32)
            expd = jnp.exp2(scores * factor)
            part = jnp.sum(expd.reshape(step // 8, 8, QUERIES), axis=0)
            total = part if total is None else total + part
            pieces.append(expd.astype(BF16))
        acc = jnp.dot(
            values[h * size : (h + 1) * size, :], jnp.concatenate(pieces, axis=0),
            preferred_element_type=F32,
        )
        outs.append(acc * (4.0 / jnp.sum(total, axis=0, keepdims=True)) * 64.0)
    return jnp.transpose(jnp.concatenate(outs, axis=0)).astype(BF16)


def mix_kernel(
    wide, narrow, x_ref, vw_ref, sw_ref, gain_ref, cols_ref, rows_ref,
    n_s, k_s, x_s, k8_s, vt_s, qt_s, kw_s, wt_s, outbox, inbox, pooled, mine,
    send_a, recv_a, send_c, recv_c, send_f, send_r, recv_r,
):
    total_vars, width = x_ref.shape
    devices = wide * narrow
    own = total_vars // devices
    per_block = QUERIES // own
    blocks = total_vars // QUERIES
    my_wide, my_narrow = lax.axis_index("wide"), lax.axis_index("narrow")
    me = my_wide * narrow + my_narrow

    def device(d):
        return {"wide": d // narrow, "narrow": lax.rem(d, narrow)}

    barrier = pltpu.get_barrier_semaphore()

    def greet(d, carry):
        @pl.when(d != me)
        def _():
            pl.semaphore_signal(barrier, inc=1, device_id=device(d), device_id_type=MESH)

        return carry

    lax.fori_loop(0, devices, greet, 0)

    size = width // HEADS
    spread = PARTS * size
    source = lax.broadcasted_iota(jnp.int32, (width, HEADS * spread), 0)
    column = lax.broadcasted_iota(jnp.int32, (width, HEADS * spread), 1)
    twice = jnp.where(source == column // spread * size + column % size, 2.0, 0.0)
    kw_s[...] = project(vw_ref[1], twice.astype(BF16))
    wt_s[0:width, :] = (jnp.transpose(vw_ref[0].astype(F32)) * 2.0).astype(BF16)
    wt_s[width : 2 * width, :] = jnp.transpose(vw_ref[2].astype(F32)).astype(BF16)
    odd = lax.broadcasted_iota(jnp.int32, (QUERIES, spread), 1) // size % 2 == 1

    def prepare(i, carry):
        rows = pl.ds(pl.multiple_of(i * QUERIES, QUERIES), QUERIES)
        normed = layer_norm(x_ref[rows, :].astype(F32), gain_ref[0:1, :])
        n_s[rows, :] = normed
        vt_s[:, rows] = (across(wt_s[width : 2 * width, :], normed) * 2.0**-8).astype(BF16)
        for h in range(HEADS):
            key = jnp.dot(normed, kw_s[:, h * spread : (h + 1) * spread], preferred_element_type=F32)
            k8_s[h, rows, :] = jnp.where(odd, low_part(key), key).astype(F8)
        return carry

    def prepare_some(i, carry):
        for u in range(PREPARE):
            prepare(i * PREPARE + u, carry)
        return carry

    lax.fori_loop(0, total_vars // QUERIES // PREPARE, prepare_some, 0)

    my_block = me // per_block

    def block_of(t):
        block, bit = 0, 1
        while bit < blocks:
            block = block + bit * lax.rem(my_block // bit + (blocks - 1 - t) // bit, 2)
            bit *= 2
        return block

    def rows_of(block):
        return pl.ds(pl.multiple_of(block * QUERIES, QUERIES), QUERIES)

    def send(d):
        pltpu.make_async_remote_copy(
            src_ref=outbox.at[d], dst_ref=inbox.at[me],
            send_sem=send_a.at[d], recv_sem=recv_a.at[me],
            device_id=device(d), device_id_type=MESH,
        ).start()

    def post(block):
        if per_block <= 4:
            for j in range(per_block):
                send(block * per_block + j)
        else:
            lax.fori_loop(0, per_block, lambda j, carry: (send(block * per_block + j), carry)[1], 0)

    def variable_block(t):
        block = block_of(t)
        rows = rows_of(block)
        out = attend_across(across(wt_s[0:width, :], n_s[rows, :]), k8_s, vt_s)
        update = jnp.dot(out, vw_ref[3], preferred_element_type=F32)
        mixed = x_ref[rows, :].astype(F32) + update
        outbox[pl.ds(block * per_block, per_block)] = mixed.reshape(per_block, own, width).astype(BF16)

    variable_block(0)
    pl.semaphore_wait(barrier, devices - 1)

    def variable_step(t, carry):
        post(block_of(t - 1))
        variable_block(t)
        return carry

    lax.fori_loop(1, blocks, variable_step, 0)

    def post_own(j, carry):
        d = my_block * per_block + j

        @pl.when(d != me)
        def _():
            send(d)

        return carry

    lax.fori_loop(0, per_block, post_own, 0)
    inbox[me] = outbox[me]
    wt_s[0:width, :] = jnp.transpose(sw_ref[0].astype(F32)).astype(BF16)
    wt_s[width : 2 * width, :] = jnp.transpose(sw_ref[2].astype(F32)).astype(BF16)

    def collect(d, carry):
        @pl.when(d != me)
        def _():
            pltpu.make_async_remote_copy(
                src_ref=outbox.at[d], dst_ref=inbox.at[d],
                send_sem=send_a.at[d], recv_sem=recv_a.at[d],
                device_id=device(d), device_id_type=MESH,
            ).wait()

        return carry

    lax.fori_loop(0, devices, collect, 0)

    tile = 8 * devices
    lump = 16 if own % 16 == 0 else 8

    tiles = lump // 8

    def prepare_samples(i):
        if lump == own:
            values = inbox[...].astype(F32)
        else:
            values = inbox[:, pl.ds(pl.multiple_of(i * lump, lump), lump), :].astype(F32)
        rows = pl.ds(pl.multiple_of(i * tiles * tile, tiles * tile), tiles * tile)
        tokens = jnp.concatenate(
            [values[:, u * 8 : u * 8 + 8, :].reshape(tile, width) for u in range(tiles)], axis=0
        )
        x_s[rows, :] = tokens.astype(BF16)
        normed = layer_norm(tokens, gain_ref[1:2, :])
        k_s[rows, :] = project(normed, sw_ref[1])
        qt_s[:, rows] = across(wt_s[0:width, :], normed).astype(BF16)
        vt_s[:, rows] = (across(wt_s[width : 2 * width, :], normed) * 2.0**-8).astype(BF16)

    pooled[...] = jnp.full(pooled.shape, -jnp.inf, F32)
    step = min(KEYS, tile)
    row_var = lax.broadcasted_iota(jnp.int32, (step, HEADS * BLOCK), 0) % 8
    col_var = lax.broadcasted_iota(jnp.int32, (step, HEADS * BLOCK), 1) % 8
    same = row_var == col_var

    def sample_chunk(c):
        rows = pl.ds(pl.multiple_of(c * BLOCK, BLOCK), BLOCK)
        base = c // (tile // BLOCK)

        def among(a, n):
            return pl.ds(pl.multiple_of(base * tile + a, BLOCK), n)

        return attend_tokens(
            qt_s[:, rows],
            lambda a, n: k_s[among(a, n), :],
            lambda a, n: vt_s[:, among(a, n)],
            tile, same,
        )

    def sample_chunks(c, count):
        out = jnp.concatenate([sample_chunk(c + u) for u in range(count)], axis=0)
        update = jnp.dot(out, sw_ref[3], preferred_element_type=F32)
        rows = pl.ds(pl.multiple_of(c * BLOCK, BLOCK), count * BLOCK)
        mixed = (x_s[rows, :].astype(F32) + update).astype(BF16).astype(F32)
        best = jnp.max(mixed.reshape(count, BLOCK // 8, 8, width), axis=1)
        for u in range(count):
            where = pl.ds(pl.multiple_of((c + u) // (tile // BLOCK) * 8, 8), 8)
            pooled[where, :] = jnp.maximum(pooled[where, :], best[u])

    piece = min(32, own)
    pieces = own // piece
    per_piece = piece * devices // BLOCK
    unroll = min(4, per_piece)
    half = devices // narrow
    target = me // half
    slot = lax.rem(me, half)
    column, pair = my_wide // 2, lax.rem(my_wide, 2)
    columns = wide // 2
    beside = {"wide": column * 2 + 1 - pair, "narrow": my_narrow}

    def piece_rows(g):
        return pl.ds(pl.multiple_of(g * piece, piece), piece)

    def to_column(w, rows, g):
        return pltpu.make_async_remote_copy(
            src_ref=mine.at[rows], dst_ref=cols_ref.at[slot, rows],
            send_sem=send_c.at[w], recv_sem=recv_c.at[slot, g],
            device_id={"wide": w * 2 + pair, "narrow": target}, device_id_type=MESH,
        )

    def to_far(w, rows):
        return pltpu.make_async_remote_copy(
            src_ref=mine.at[rows], dst_ref=cols_ref.at[slot, rows],
            send_sem=send_c.at[columns + 1 + w], recv_sem=recv_c.at[slot, 0],
            device_id={"wide": w * 2 + 1 - pair, "narrow": target}, device_id_type=MESH,
        )

    def to_pair(rows):
        return pltpu.make_async_remote_copy(
            src_ref=mine.at[rows], dst_ref=cols_ref.at[slot, rows],
            send_sem=send_c.at[columns], recv_sem=recv_c.at[slot, 0],
            device_id={"wide": column * 2 + 1 - pair, "narrow": target}, device_id_type=MESH,
        )

    def to_row(n, rows):
        return pltpu.make_async_remote_copy(
            src_ref=mine.at[rows], dst_ref=rows_ref.at[my_narrow, rows],
            send_sem=send_r.at[n], recv_sem=recv_r.at[my_narrow],
            device_id={"wide": my_wide, "narrow": n}, device_id_type=MESH,
        )

    def forward(i, rows):
        return pltpu.make_async_remote_copy(
            src_ref=cols_ref.at[i, rows], dst_ref=cols_ref.at[i, rows],
            send_sem=send_f.at[i], recv_sem=recv_c.at[i, 0],
            device_id=beside, device_id_type=MESH,
        )

    def arrival(i, rows, g):
        return pltpu.make_async_remote_copy(
            src_ref=cols_ref.at[i, rows], dst_ref=cols_ref.at[i, rows],
            send_sem=send_f.at[i], recv_sem=recv_c.at[i, g],
            device_id=beside, device_id_type=MESH,
        )

    def column_copies(do, rows, g):
        def one(w, carry):
            @pl.when(w != column)
            def _():
                do(to_column(w, rows, g))

            return carry

        lax.fori_loop(0, columns, one, 0)

    def far_copies(do):
        rows = piece_rows(pieces - 1)

        def one(w, carry):
            @pl.when(w != column)
            def _():
                do(to_far(w, rows))

            return carry

        lax.fori_loop(0, columns, one, 0)

    def chip_copies(do, rows):
        do(to_pair(rows))

        @pl.when(target != my_narrow)
        def _():
            do(to_column(column, rows, 0))

        def other(n, carry):
            @pl.when(n != my_narrow)
            def _():
                do(to_row(n, rows))

            return carry

        lax.fori_loop(0, narrow, other, 0)

    def each_source(do):
        def one(i, carry):
            from_wide = (my_narrow * half + i) // narrow
            passes_here = (lax.rem(from_wide, 2) == pair) & (from_wide // 2 != column)

            @pl.when(passes_here)
            def _():
                do(i)

            return carry

        lax.fori_loop(0, half, one, 0)

    def pass_on(g):
        rows = piece_rows(g)

        def one(i):
            arrival(i, rows, g).wait_recv()
            forward(i, rows).start()

        each_source(one)

    def prepare_piece(g):
        for i in range(piece // lump):
            prepare_samples(g * (piece // lump) + i)

    def sample_piece(g, following):
        def group(i, inner):
            sample_chunks(g * per_piece + i * unroll, unroll)
            return inner

        if per_piece == unroll:
            group(0, 0)
        else:
            lax.fori_loop(0, per_piece // unroll, group, 0)
        if following:
            prepare_piece(g + 1)
        rows = piece_rows(g)
        best = layer_norm(pooled[rows, :], gain_ref[2:3, :])
        mine[rows, :] = best
        rows_ref[my_narrow, rows, :] = best

        @pl.when(target == my_narrow)
        def _():
            cols_ref[slot, rows, :] = best

        column_copies(lambda copy: copy.start(), rows, g)
        chip_copies(lambda copy: copy.start(), rows)

    def sample_step(g, carry):
        sample_piece(g, True)

        @pl.when(g >= LAG)
        def _():
            pass_on(g - LAG)

        return carry

    prepare_piece(0)
    if pieces > 1:
        lax.fori_loop(0, pieces - 1, sample_step, 0)
    sample_piece(pieces - 1, False)
    far_copies(lambda copy: copy.start())
    lax.fori_loop(max(pieces - 1 - LAG, 0), pieces - 1, lambda g, carry: (pass_on(g), carry)[1], 0)
    each_source(lambda i: arrival(i, piece_rows(pieces - 1), pieces - 1).wait_recv())
    whole = pl.ds(0, own)

    def arrived(i, carry):
        from_wide = (my_narrow * half + i) // narrow
        passes_here = (lax.rem(from_wide, 2) == pair) & (from_wide // 2 != column)

        @pl.when(jnp.logical_not(passes_here) & (my_narrow * half + i != me))
        def _():
            arrival(i, whole, 0).wait_recv()

        return carry

    lax.fori_loop(0, half, arrived, 0)

    def row_arrived(n, carry):
        @pl.when(n != my_narrow)
        def _():
            pltpu.make_async_remote_copy(
                src_ref=mine, dst_ref=rows_ref.at[n], send_sem=send_r.at[0],
                recv_sem=recv_r.at[n], device_id=beside, device_id_type=MESH,
            ).wait_recv()

        return carry

    lax.fori_loop(0, narrow, row_arrived, 0)
    column_copies(lambda copy: copy.wait_send(), whole, 0)
    chip_copies(lambda copy: copy.wait_send(), whole)
    far_copies(lambda copy: copy.wait_send())
    if pieces > 1:
        each_source(lambda i: forward(i, pl.ds(0, (pieces - 1) * piece)).wait_send())


def edge_kernel(tile, rows_ref, cols_ref, w_ref, none_ref, out_ref, held, sem):
    width = rows_ref.shape[1]
    scale = 1.0 / width**0.5
    none = jnp.broadcast_to(none_ref[...][None, :], (16, width))
    rows = rows_ref[...]
    src = project(rows, w_ref[0])
    dst = project(rows, w_ref[1])
    none_rows = across(rows, none).astype(BF16).astype(F32)[:, 0:1]
    copies = []
    for i in range(0, cols_ref.shape[0], tile):
        cols = cols_ref[i : i + tile, :]
        forward = jnp.exp(across(src, project(cols, w_ref[1])) * scale)
        backward = jnp.exp(across(dst, project(cols, w_ref[0])) * scale)
        none_cols = across(none, cols).astype(BF16).astype(F32)
        absent = jnp.exp(none_rows + none_cols[0:1, :])
        total = forward + backward + absent
        lanes = pl.ds(i, tile)
        held[0, :, lanes] = forward / total
        held[1, :, lanes] = backward / total
        held[2, :, lanes] = absent / total
        copies.append(
            pltpu.make_async_copy(held.at[:, :, lanes], out_ref.at[:, :, lanes], sem.at[i // tile])
        )
        copies[-1].start()
    for copy in copies:
        copy.wait()


def on_device(states, var_weights, samp_weights, norm_gains, edge_weights, none_weight):
    total_vars, samp_local, width = states.shape
    wide, narrow = lax.axis_size("wide"), lax.axis_size("narrow")
    devices = wide * narrow
    own = total_vars // devices
    assert samp_local == 1 and BLOCK % own == 0 and own % 8 == 0
    half = devices // narrow
    assert narrow == 2 and wide % 2 == 0 and half % 4 == 0
    spread = PARTS * (width // HEADS)
    piece = min(32, own)
    vmem = pl.BlockSpec(memory_space=pltpu.VMEM)
    dma = pltpu.SemaphoreType.DMA
    cols, rows = pl.pallas_call(
        functools.partial(mix_kernel, wide, narrow),
        out_shape=(
            jax.ShapeDtypeStruct((half, own, width), BF16),
            jax.ShapeDtypeStruct((narrow, own, width), BF16),
        ),
        in_specs=[vmem] * 4,
        out_specs=(vmem, vmem),
        scratch_shapes=[pltpu.VMEM((total_vars, width), BF16)] * 3
        + [
            pltpu.VMEM((HEADS, total_vars, spread), F8),
            pltpu.VMEM((width, total_vars), BF16),
            pltpu.VMEM((width, total_vars), BF16),
            pltpu.VMEM((width, HEADS * spread), BF16),
            pltpu.VMEM((2 * width, width), BF16),
            pltpu.VMEM((devices, own, width), BF16),
            pltpu.VMEM((devices, own, width), BF16),
            pltpu.VMEM((own, width), F32),
            pltpu.VMEM((own, width), BF16),
            dma((devices,)), dma((devices,)), dma((wide + 1,)), dma((half, own // piece)),
            dma((half,)), dma((narrow,)), dma((narrow,)),
        ],
        compiler_params=pltpu.CompilerParams(
            collective_id=0, has_side_effects=True, vmem_limit_bytes=60 * 2**20
        ),
        name="mix",
    )(states.reshape(total_vars, width), var_weights, samp_weights, norm_gains)
    cols = cols.reshape(half * own, width)
    rows = rows.reshape(narrow * own, width)
    row_count, col_count = narrow * own, half * own
    tile = min(256, col_count)
    return pl.pallas_call(
        functools.partial(edge_kernel, tile),
        out_shape=jax.ShapeDtypeStruct((3, row_count, col_count), F32),
        in_specs=[vmem] * 4,
        out_specs=pl.BlockSpec(memory_space=pl.ANY),
        scratch_shapes=[pltpu.VMEM((3, row_count, col_count), F32), dma((col_count // tile,))],
        name="edge",
    )(rows, cols, edge_weights, none_weight)


def solution(mesh):
    return jax.shard_map(
        on_device,
        mesh=mesh,
        in_specs=(P(None, ("groups", "wide", "narrow"), None), P(), P(), P(), P(), P()),
        out_specs=P("groups", "wide", "narrow"),
        check_vma=False,
    )
```

```python
import functools
import math

import jax
import jax.numpy as jnp
from jax import lax
from jax.experimental import pallas as pl
from jax.experimental.pallas import tpu as pltpu
from jax.sharding import PartitionSpec as P

HEADS = 8
BLOCK = 128
QUERIES = 256
KEYS = 256
ACROSS = 2048
F32, BF16, F8 = jnp.float32, jnp.bfloat16, jnp.float8_e4m3fn
PARTS = 4
PREPARE = 8
LAG = 2
MESH = pl.DeviceIdType.MESH


def layer_norm(values, gain):
    mean = jnp.mean(values, axis=-1, keepdims=True)
    centered = values - mean
    var = jnp.mean(centered * centered, axis=-1, keepdims=True)
    return (centered * lax.rsqrt(var + 1e-05) * gain).astype(BF16)


def project(normed, weight):
    return jnp.dot(normed, weight, preferred_element_type=F32).astype(BF16)


def across(a, b):
    return lax.dot_general(a, b, (((1,), (1,)), ((), ())), preferred_element_type=F32)


def attend_tokens(q, keys_of, values_of, length, same):
    width, tokens = q.shape
    size = width // HEADS
    step = min(KEYS, length)
    factor = math.log2(math.e) / math.sqrt(size)
    blank = jnp.zeros((size, tokens), BF16)
    stacked = jnp.concatenate(
        [
            jnp.concatenate([q[i * size : (i + 1) * size] if i == h else blank for h in range(HEADS)], axis=1)
            for i in range(HEADS)
        ],
        axis=0,
    )
    accs, total = None, None
    for j in range(0, length, step):
        scores = jnp.dot(keys_of(j, step), stacked, preferred_element_type=F32)
        expd = jnp.where(same, jnp.exp2(scores * factor), 0.0)
        part = jnp.sum(expd.reshape(step // 8, 8, HEADS * tokens), axis=0)
        total = part if total is None else total + part
        expd = expd.astype(BF16)
        values = values_of(j, step)
        terms = [
            jnp.dot(
                values[h * size : (h + 1) * size], expd[:, h * tokens : (h + 1) * tokens],
                preferred_element_type=F32,
            )
            for h in range(HEADS)
        ]
        accs = terms if accs is None else [acc + term for acc, term in zip(accs, terms)]
    inverse = 4.0 / jnp.sum(total, axis=0, keepdims=True)
    outs = [acc * inverse[:, h * tokens : (h + 1) * tokens] * 64.0 for h, acc in enumerate(accs)]
    return jnp.transpose(jnp.concatenate(outs, axis=0)).astype(BF16)


def low_part(values):
    return values - values.astype(F8).astype(F32)


def attend_across(q, keys, values):
    width, length = values.shape
    size = width // HEADS
    step = min(ACROSS, length)
    factor = math.log2(math.e) / math.sqrt(size) / 4.0
    outs = []
    for h in range(HEADS):
        part = q[h * size : (h + 1) * size, :]
        high, low = part.astype(F8), low_part(part).astype(F8)
        stacked = jnp.concatenate([high, high, low, low], axis=0)
        pieces, total = [], None
        for j in range(0, length, step):
            scores = jnp.dot(keys[h, j : j + step, :], stacked, preferred_element_type=F32)
            expd = jnp.exp2(scores * factor)
            part = jnp.sum(expd.reshape(step // 8, 8, QUERIES), axis=0)
            total = part if total is None else total + part
            pieces.append(expd.astype(BF16))
        acc = jnp.dot(
            values[h * size : (h + 1) * size, :], jnp.concatenate(pieces, axis=0),
            preferred_element_type=F32,
        )
        outs.append(acc * (4.0 / jnp.sum(total, axis=0, keepdims=True)) * 64.0)
    return jnp.transpose(jnp.concatenate(outs, axis=0)).astype(BF16)


def mix_kernel(
    wide, narrow, x_ref, vw_ref, sw_ref, gain_ref, cols_ref, rows_ref,
    n_s, k_s, x_s, k8_s, vt_s, qt_s, kw_s, wt_s, outbox, inbox, pooled, mine,
    send_a, recv_a, send_c, recv_c, send_f, send_r, recv_r,
):
    total_vars, width = x_ref.shape
    devices = wide * narrow
    own = total_vars // devices
    per_block = QUERIES // own
    blocks = total_vars // QUERIES
    my_wide, my_narrow = lax.axis_index("wide"), lax.axis_index("narrow")
    me = my_wide * narrow + my_narrow

    def device(d):
        return {"wide": d // narrow, "narrow": lax.rem(d, narrow)}

    barrier = pltpu.get_barrier_semaphore()

    def greet(d, carry):
        @pl.when(d != me)
        def _():
            pl.semaphore_signal(barrier, inc=1, device_id=device(d), device_id_type=MESH)

        return carry

    lax.fori_loop(0, devices, greet, 0)

    size = width // HEADS
    spread = PARTS * size
    source = lax.broadcasted_iota(jnp.int32, (width, HEADS * spread), 0)
    column = lax.broadcasted_iota(jnp.int32, (width, HEADS * spread), 1)
    twice = jnp.where(source == column // spread * size + column % size, 2.0, 0.0)
    kw_s[...] = project(vw_ref[1], twice.astype(BF16))
    wt_s[0:width, :] = (jnp.transpose(vw_ref[0].astype(F32)) * 2.0).astype(BF16)
    wt_s[width : 2 * width, :] = jnp.transpose(vw_ref[2].astype(F32)).astype(BF16)
    odd = lax.broadcasted_iota(jnp.int32, (QUERIES, spread), 1) // size % 2 == 1

    def prepare(i, carry):
        rows = pl.ds(pl.multiple_of(i * QUERIES, QUERIES), QUERIES)
        normed = layer_norm(x_ref[rows, :].astype(F32), gain_ref[0:1, :])
        n_s[rows, :] = normed
        vt_s[:, rows] = (across(wt_s[width : 2 * width, :], normed) * 2.0**-8).astype(BF16)
        for h in range(HEADS):
            key = jnp.dot(normed, kw_s[:, h * spread : (h + 1) * spread], preferred_element_type=F32)
            k8_s[h, rows, :] = jnp.where(odd, low_part(key), key).astype(F8)
        return carry

    def prepare_some(i, carry):
        for u in range(PREPARE):
            prepare(i * PREPARE + u, carry)
        return carry

    lax.fori_loop(0, total_vars // QUERIES // PREPARE, prepare_some, 0)

    my_block = me // per_block

    def block_of(t):
        block, bit = 0, 1
        while bit < blocks:
            block = block + bit * lax.rem(my_block // bit + (blocks - 1 - t) // bit, 2)
            bit *= 2
        return block

    def rows_of(block):
        return pl.ds(pl.multiple_of(block * QUERIES, QUERIES), QUERIES)

    def send(d):
        pltpu.make_async_remote_copy(
            src_ref=outbox.at[d], dst_ref=inbox.at[me],
            send_sem=send_a.at[d], recv_sem=recv_a.at[me],
            device_id=device(d), device_id_type=MESH,
        ).start()

    def post(block):
        if per_block <= 4:
            for j in range(per_block):
                send(block * per_block + j)
        else:
            lax.fori_loop(0, per_block, lambda j, carry: (send(block * per_block + j), carry)[1], 0)

    def variable_block(t):
        block = block_of(t)
        rows = rows_of(block)
        out = attend_across(across(wt_s[0:width, :], n_s[rows, :]), k8_s, vt_s)
        update = jnp.dot(out, vw_ref[3], preferred_element_type=F32)
        mixed = x_ref[rows, :].astype(F32) + update
        outbox[pl.ds(block * per_block, per_block)] = mixed.reshape(per_block, own, width).astype(BF16)

    variable_block(0)
    pl.semaphore_wait(barrier, devices - 1)

    def variable_step(t, carry):
        post(block_of(t - 1))
        variable_block(t)
        return carry

    lax.fori_loop(1, blocks, variable_step, 0)

    def post_own(j, carry):
        d = my_block * per_block + j

        @pl.when(d != me)
        def _():
            send(d)

        return carry

    lax.fori_loop(0, per_block, post_own, 0)
    inbox[me] = outbox[me]
    wt_s[0:width, :] = jnp.transpose(sw_ref[0].astype(F32)).astype(BF16)
    wt_s[width : 2 * width, :] = jnp.transpose(sw_ref[2].astype(F32)).astype(BF16)

    def collect(d, carry):
        @pl.when(d != me)
        def _():
            pltpu.make_async_remote_copy(
                src_ref=outbox.at[d], dst_ref=inbox.at[d],
                send_sem=send_a.at[d], recv_sem=recv_a.at[d],
                device_id=device(d), device_id_type=MESH,
            ).wait()

        return carry

    lax.fori_loop(0, devices, collect, 0)

    tile = 8 * devices
    lump = 16 if own % 16 == 0 else 8

    tiles = lump // 8

    def prepare_samples(i):
        if lump == own:
            values = inbox[...].astype(F32)
        else:
            values = inbox[:, pl.ds(pl.multiple_of(i * lump, lump), lump), :].astype(F32)
        rows = pl.ds(pl.multiple_of(i * tiles * tile, tiles * tile), tiles * tile)
        tokens = jnp.concatenate(
            [values[:, u * 8 : u * 8 + 8, :].reshape(tile, width) for u in range(tiles)], axis=0
        )
        x_s[rows, :] = tokens.astype(BF16)
        normed = layer_norm(tokens, gain_ref[1:2, :])
        k_s[rows, :] = project(normed, sw_ref[1])
        qt_s[:, rows] = across(wt_s[0:width, :], normed).astype(BF16)
        vt_s[:, rows] = (across(wt_s[width : 2 * width, :], normed) * 2.0**-8).astype(BF16)

    pooled[...] = jnp.full(pooled.shape, -jnp.inf, F32)
    step = min(KEYS, tile)
    row_var = lax.broadcasted_iota(jnp.int32, (step, HEADS * BLOCK), 0) % 8
    col_var = lax.broadcasted_iota(jnp.int32, (step, HEADS * BLOCK), 1) % 8
    same = row_var == col_var

    def sample_chunk(c):
        rows = pl.ds(pl.multiple_of(c * BLOCK, BLOCK), BLOCK)
        base = c // (tile // BLOCK)

        def among(a, n):
            return pl.ds(pl.multiple_of(base * tile + a, BLOCK), n)

        return attend_tokens(
            qt_s[:, rows],
            lambda a, n: k_s[among(a, n), :],
            lambda a, n: vt_s[:, among(a, n)],
            tile, same,
        )

    def sample_chunks(c, count):
        out = jnp.concatenate([sample_chunk(c + u) for u in range(count)], axis=0)
        update = jnp.dot(out, sw_ref[3], preferred_element_type=F32)
        rows = pl.ds(pl.multiple_of(c * BLOCK, BLOCK), count * BLOCK)
        mixed = (x_s[rows, :].astype(F32) + update).astype(BF16).astype(F32)
        best = jnp.max(mixed.reshape(count, BLOCK // 8, 8, width), axis=1)
        for u in range(count):
            where = pl.ds(pl.multiple_of((c + u) // (tile // BLOCK) * 8, 8), 8)
            pooled[where, :] = jnp.maximum(pooled[where, :], best[u])

    piece = min(32, own)
    pieces = own // piece
    per_piece = piece * devices // BLOCK
    unroll = min(4, per_piece)
    half = devices // narrow
    target = me // half
    slot = lax.rem(me, half)
    column, pair = my_wide // 2, lax.rem(my_wide, 2)
    columns = wide // 2
    beside = {"wide": column * 2 + 1 - pair, "narrow": my_narrow}

    def piece_rows(g):
        return pl.ds(pl.multiple_of(g * piece, piece), piece)

    def to_column(w, rows, g):
        return pltpu.make_async_remote_copy(
            src_ref=mine.at[rows], dst_ref=cols_ref.at[slot, rows],
            send_sem=send_c.at[w], recv_sem=recv_c.at[slot, g],
            device_id={"wide": w * 2 + pair, "narrow": target}, device_id_type=MESH,
        )

    def to_far(w, rows):
        return pltpu.make_async_remote_copy(
            src_ref=mine.at[rows], dst_ref=cols_ref.at[slot, rows],
            send_sem=send_c.at[columns + 1 + w], recv_sem=recv_c.at[slot, 0],
            device_id={"wide": w * 2 + 1 - pair, "narrow": target}, device_id_type=MESH,
        )

    def to_pair(rows):
        return pltpu.make_async_remote_copy(
            src_ref=mine.at[rows], dst_ref=cols_ref.at[slot, rows],
            send_sem=send_c.at[columns], recv_sem=recv_c.at[slot, 0],
            device_id={"wide": column * 2 + 1 - pair, "narrow": target}, device_id_type=MESH,
        )

    def to_row(n, rows):
        return pltpu.make_async_remote_copy(
            src_ref=mine.at[rows], dst_ref=rows_ref.at[my_narrow, rows],
            send_sem=send_r.at[n], recv_sem=recv_r.at[my_narrow],
            device_id={"wide": my_wide, "narrow": n}, device_id_type=MESH,
        )

    def forward(i, rows):
        return pltpu.make_async_remote_copy(
            src_ref=cols_ref.at[i, rows], dst_ref=cols_ref.at[i, rows],
            send_sem=send_f.at[i], recv_sem=recv_c.at[i, 0],
            device_id=beside, device_id_type=MESH,
        )

    def arrival(i, rows, g):
        return pltpu.make_async_remote_copy(
            src_ref=cols_ref.at[i, rows], dst_ref=cols_ref.at[i, rows],
            send_sem=send_f.at[i], recv_sem=recv_c.at[i, g],
            device_id=beside, device_id_type=MESH,
        )

    def column_copies(do, rows, g):
        def one(k, carry):
            w = jnp.where(column < columns // 2, columns - 1 - k, k)

            @pl.when(w != column)
            def _():
                do(to_column(w, rows, g))

            return carry

        lax.fori_loop(0, columns, one, 0)

    def far_copies(do):
        rows = piece_rows(pieces - 1)

        def one(w, carry):
            @pl.when(w != column)
            def _():
                do(to_far(w, rows))

            return carry

        lax.fori_loop(0, columns, one, 0)

    def chip_copies(do, rows):
        do(to_pair(rows))

        @pl.when(target != my_narrow)
        def _():
            do(to_column(column, rows, 0))

        def other(n, carry):
            @pl.when(n != my_narrow)
            def _():
                do(to_row(n, rows))

            return carry

        lax.fori_loop(0, narrow, other, 0)

    def each_source(do):
        def one(i, carry):
            from_wide = (my_narrow * half + i) // narrow
            passes_here = (lax.rem(from_wide, 2) == pair) & (from_wide // 2 != column)

            @pl.when(passes_here)
            def _():
                do(i)

            return carry

        lax.fori_loop(0, half, one, 0)

    def pass_on(g):
        rows = piece_rows(g)

        def one(i):
            arrival(i, rows, g).wait_recv()
            forward(i, rows).start()

        each_source(one)

    def prepare_piece(g):
        for i in range(piece // lump):
            prepare_samples(g * (piece // lump) + i)

    def sample_piece(g, following):
        def group(i, inner):
            sample_chunks(g * per_piece + i * unroll, unroll)
            return inner

        if per_piece == unroll:
            group(0, 0)
        else:
            lax.fori_loop(0, per_piece // unroll, group, 0)
        if following:
            prepare_piece(g + 1)
        rows = piece_rows(g)
        best = layer_norm(pooled[rows, :], gain_ref[2:3, :])
        mine[rows, :] = best
        rows_ref[my_narrow, rows, :] = best

        @pl.when(target == my_narrow)
        def _():
            cols_ref[slot, rows, :] = best

        column_copies(lambda copy: copy.start(), rows, g)
        chip_copies(lambda copy: copy.start(), rows)

    def sample_step(g, carry):
        sample_piece(g, True)

        @pl.when(g >= LAG)
        def _():
            pass_on(g - LAG)

        return carry

    prepare_piece(0)
    if pieces > 1:
        lax.fori_loop(0, pieces - 1, sample_step, 0)
    sample_piece(pieces - 1, False)
    far_copies(lambda copy: copy.start())
    lax.fori_loop(max(pieces - 1 - LAG, 0), pieces - 1, lambda g, carry: (pass_on(g), carry)[1], 0)
    each_source(lambda i: arrival(i, piece_rows(pieces - 1), pieces - 1).wait_recv())
    whole = pl.ds(0, own)

    def arrived(i, carry):
        from_wide = (my_narrow * half + i) // narrow
        passes_here = (lax.rem(from_wide, 2) == pair) & (from_wide // 2 != column)

        @pl.when(jnp.logical_not(passes_here) & (my_narrow * half + i != me))
        def _():
            arrival(i, whole, 0).wait_recv()

        return carry

    lax.fori_loop(0, half, arrived, 0)

    def row_arrived(n, carry):
        @pl.when(n != my_narrow)
        def _():
            pltpu.make_async_remote_copy(
                src_ref=mine, dst_ref=rows_ref.at[n], send_sem=send_r.at[0],
                recv_sem=recv_r.at[n], device_id=beside, device_id_type=MESH,
            ).wait_recv()

        return carry

    lax.fori_loop(0, narrow, row_arrived, 0)
    column_copies(lambda copy: copy.wait_send(), whole, 0)
    chip_copies(lambda copy: copy.wait_send(), whole)
    far_copies(lambda copy: copy.wait_send())
    if pieces > 1:
        each_source(lambda i: forward(i, pl.ds(0, (pieces - 1) * piece)).wait_send())


def edge_kernel(tile, rows_ref, cols_ref, w_ref, none_ref, out_ref, held, sem):
    width = rows_ref.shape[1]
    scale = 1.0 / width**0.5
    none = jnp.broadcast_to(none_ref[...][None, :], (16, width))
    rows = rows_ref[...]
    src = project(rows, w_ref[0])
    dst = project(rows, w_ref[1])
    none_rows = across(rows, none).astype(BF16).astype(F32)[:, 0:1]
    copies = []
    for i in range(0, cols_ref.shape[0], tile):
        cols = cols_ref[i : i + tile, :]
        forward = jnp.exp(across(src, project(cols, w_ref[1])) * scale)
        backward = jnp.exp(across(dst, project(cols, w_ref[0])) * scale)
        none_cols = across(none, cols).astype(BF16).astype(F32)
        absent = jnp.exp(none_rows + none_cols[0:1, :])
        total = forward + backward + absent
        lanes = pl.ds(i, tile)
        held[0, :, lanes] = forward / total
        held[1, :, lanes] = backward / total
        held[2, :, lanes] = absent / total
        copies.append(
            pltpu.make_async_copy(held.at[:, :, lanes], out_ref.at[:, :, lanes], sem.at[i // tile])
        )
        copies[-1].start()
    for copy in copies:
        copy.wait()


def on_device(states, var_weights, samp_weights, norm_gains, edge_weights, none_weight):
    total_vars, samp_local, width = states.shape
    wide, narrow = lax.axis_size("wide"), lax.axis_size("narrow")
    devices = wide * narrow
    own = total_vars // devices
    assert samp_local == 1 and BLOCK % own == 0 and own % 8 == 0
    half = devices // narrow
    assert narrow == 2 and wide % 2 == 0 and half % 4 == 0
    spread = PARTS * (width // HEADS)
    piece = min(32, own)
    vmem = pl.BlockSpec(memory_space=pltpu.VMEM)
    dma = pltpu.SemaphoreType.DMA
    cols, rows = pl.pallas_call(
        functools.partial(mix_kernel, wide, narrow),
        out_shape=(
            jax.ShapeDtypeStruct((half, own, width), BF16),
            jax.ShapeDtypeStruct((narrow, own, width), BF16),
        ),
        in_specs=[vmem] * 4,
        out_specs=(vmem, vmem),
        scratch_shapes=[pltpu.VMEM((total_vars, width), BF16)] * 3
        + [
            pltpu.VMEM((HEADS, total_vars, spread), F8),
            pltpu.VMEM((width, total_vars), BF16),
            pltpu.VMEM((width, total_vars), BF16),
            pltpu.VMEM((width, HEADS * spread), BF16),
            pltpu.VMEM((2 * width, width), BF16),
            pltpu.VMEM((devices, own, width), BF16),
            pltpu.VMEM((devices, own, width), BF16),
            pltpu.VMEM((own, width), F32),
            pltpu.VMEM((own, width), BF16),
            dma((devices,)), dma((devices,)), dma((wide + 1,)), dma((half, own // piece)),
            dma((half,)), dma((narrow,)), dma((narrow,)),
        ],
        compiler_params=pltpu.CompilerParams(
            collective_id=0, has_side_effects=True, vmem_limit_bytes=60 * 2**20
        ),
        name="mix",
    )(states.reshape(total_vars, width), var_weights, samp_weights, norm_gains)
    cols = cols.reshape(half * own, width)
    rows = rows.reshape(narrow * own, width)
    row_count, col_count = narrow * own, half * own
    tile = min(256, col_count)
    return pl.pallas_call(
        functools.partial(edge_kernel, tile),
        out_shape=jax.ShapeDtypeStruct((3, row_count, col_count), F32),
        in_specs=[vmem] * 4,
        out_specs=pl.BlockSpec(memory_space=pl.ANY),
        scratch_shapes=[pltpu.VMEM((3, row_count, col_count), F32), dma((col_count // tile,))],
        name="edge",
    )(rows, cols, edge_weights, none_weight)


def solution(mesh):
    return jax.shard_map(
        on_device,
        mesh=mesh,
        in_specs=(P(None, ("groups", "wide", "narrow"), None), P(), P(), P(), P(), P()),
        out_specs=P("groups", "wide", "narrow"),
        check_vma=False,
    )
```
